32 devices in a mesh: obs: 8 (over z, y), lvl: 4 (over x, core).
Axes of the slice: x: 2, y: 2, z: 4, core: 2. Of those that a mesh axis runs over, the one named last changes fastest.
Arguments:
- rhs: float32 [64, 262144], P(None, ('obs', 'lvl')), may hold values from -15 to 15
- tile_weights: bfloat16 [4096, 64, 128], P(('obs', 'lvl')), may hold values from -0.3125 to 0.3125
- tile_owner: int32 [4096, 1], P(('obs', 'lvl')), may hold values from 0 to 31; in each aligned block of 128 rows (0 to 127, 128 to 255, ...) at most 8 rows name the same one
- tile_row: int32 [4096], P(('obs', 'lvl')), may hold values from 0 to 31
- axis_a: bfloat16 [128, 8, 128], P('obs', 'lvl'), as said below
- axis_b: bfloat16 [8, 128, 128], P('lvl'), as said below
- coupling: float32 [8, 8], replicated, as said below
- noise: float32 [64], replicated, may hold values from 0.1 to 1
Outputs:
- solution: float32 [64, 262144], P(None, ('obs', 'lvl'))
- residual: float32 [64, 262144], P(None, ('obs', 'lvl'))
The draws below stay inside these ranges and needn't reach their ends.
Inputs may be any that keep to these rules, and one draw needn't show every extreme that they name: `tile_owner`: among the 128 tiles of one device no owner is named more than 8 times, a bound that some block reaches. For each level l, axis_a[x, l, a] equals axis_a[a, l, x]. For each level l, axis_b[l] is symmetric. coupling is symmetric and positive definite.
All inputs are finite; a program needn't handle non-finite values.
Results may differ from the reference program's by a relative error of at most 0.017.
Values may be sent and summed in bfloat16 or wider, within the bound.
No kernel may reach another device: no remote copies, remote signals or barrier semaphores. Data moves between devices by JAX's collectives and lax.ppermute only.
A program may use at most 64 MiB of HBM per device.

```python
import math
import jax
import jax.numpy as jnp
import numpy as np
from jax import lax

R = 64
TB = 64
NB = 128
NA = 128
LEVELS = 8
ITERS = 2
TILE_DEV = 128
NTILES = 4096
NOBS = 262144
CAP = 8
BLK_DEV = 32
N_OBS = 8
N_LVL = 4
DEVICES = 32


def symmetric_stack(raw, diag_key, count, order):
    sym = (raw + jnp.swapaxes(raw, 1, 2)) * (0.5 / jnp.sqrt(2.0 * order))
    diagonal = jax.random.uniform(diag_key, (count, order), jnp.float32, 1.0, 2.0)
    return sym + diagonal[:, :, None] * jnp.eye(order, dtype=jnp.float32)[None]


def draw_rhs(key, part):
    base_key = jax.random.fold_in(key, 53)
    place = jnp.arange(NOBS, dtype=jnp.float32) / NOBS
    raw = jnp.clip(jax.random.normal(base_key, (R, NOBS), jnp.float32), -6.0, 6.0)
    scale = 0.4 * jnp.exp(jnp.log(6.0) * place)
    return raw * scale[None, :]


def draw_axis_a(key, part):
    first_key, second_key = jax.random.split(jax.random.fold_in(key, 11))
    raw = jax.random.normal(first_key, (LEVELS, NA, NA), jnp.float32)
    stack = symmetric_stack(raw, second_key, LEVELS, NA)
    return jnp.transpose(stack, (1, 0, 2)).astype(jnp.bfloat16)


def draw_axis_b(key, part):
    first_key, second_key = jax.random.split(jax.random.fold_in(key, 23))
    raw = jax.random.normal(first_key, (LEVELS, NB, NB), jnp.float32)
    return symmetric_stack(raw, second_key, LEVELS, NB).astype(jnp.bfloat16)


def draw_coupling(key, part):
    inner = jax.random.normal(jax.random.fold_in(key, 37), (LEVELS, LEVELS), jnp.float32)
    return 0.5 * jnp.eye(LEVELS, dtype=jnp.float32) + jnp.dot(inner, inner.T) / LEVELS


def touch_ends(entries, stream_key, smallest, top_value):
    longest = entries.shape.index(max(entries.shape))
    spots = []
    for shift in (0, 1):
        where = [jax.random.randint(jax.random.fold_in(stream_key, axis), (), 0, length) for axis, length in enumerate(entries.shape)]
        where[longest] = (where[longest] + shift) % entries.shape[longest]
        spots.append(tuple(where))
    return entries.at[spots[0]].set(smallest).at[spots[1]].set(top_value)


def block_levels(own_key, dims, cuts, smallest, largest):
    def one(position, blocks):
        steps = jax.random.uniform(jax.random.fold_in(jax.random.fold_in(own_key, 6), position), (blocks,), jnp.float32, smallest / len(cuts), largest / len(cuts))
        return jnp.repeat(jnp.exp(steps), dims[position] // blocks).reshape((-1,) + (1,) * (len(dims) - position - 1))

    factor_of = one(*cuts[0])
    for cut in cuts[1:]:
        factor_of = factor_of * one(*cut)
    return factor_of


def routed_block(stream_key, own, number, rows, count, top, limit, slope):
    ranking = jax.random.permutation(stream_key, count)
    packed, common = shares(count, rows * top, limit, slope, True), shares(count, rows * top, limit, slope, False)
    places = jnp.arange(count)

    def named(tallies, rotation):
        used = int((tallies > 0).sum())
        fixed = max(1, used // 4)
        shifted = fixed + (places - fixed + rotation * (used - fixed)) % max(1, count - fixed)
        return jnp.zeros((count,), jnp.int32).at[ranking[jnp.where(places < fixed, places, shifted)]].set(jnp.asarray(tallies, jnp.int32))

    tallies = jnp.where(number % 4 == 0, named(packed, number // 4), named(common, number - number // 4 - 1))
    mixed = jax.random.permutation(jax.random.fold_in(own, 3), count)
    source_of, receiver = mixed[0:count // 2 * 2:2], mixed[1:count // 2 * 2:2]
    room = jnp.minimum(tallies[source_of] - 1, limit - tallies[receiver]) // 2
    room = jnp.where((source_of == ranking[0]) | (receiver == ranking[0]) | (tallies[receiver] == 0), 0, jnp.maximum(room, 0))
    shifted = jax.random.randint(jax.random.fold_in(own, 4), (count // 2,), 0, 1 << 20) % (room + 1)
    tallies = tallies.at[source_of].add(-shifted).at[receiver].add(shifted)
    members = jnp.searchsorted(jnp.cumsum(tallies), jnp.arange(rows * top), side="right").astype(jnp.int32)
    listing = members.reshape(top, rows).T
    listing = listing[jax.random.permutation(jax.random.fold_in(own, 1), rows)]
    rotation = jax.random.randint(jax.random.fold_in(own, 2), (rows, 1), 0, top)
    return jnp.take_along_axis(listing, (jnp.arange(top)[None, :] + rotation) % top, axis=1)


def shares(number_of, total, bound, slope, full):
    loads = [(1 << 20) // math.isqrt(rank ** slope) + 1 for rank in range(1, number_of + 1)]
    largest = bound if full else min(bound, max(-(-total // number_of), total * loads[0] // sum(loads)))
    least = 1 if total - largest >= number_of - 1 else 0
    given, rest = [largest] + [least] * (number_of - 1), total - largest - least * (number_of - 1)
    while rest > 0:
        movable = [i for i in range(1, number_of) if given[i] < largest] or [i for i in range(1, number_of) if given[i] < bound]
        mass, budget = sum([loads[i] for i in movable]), rest
        for i in movable:
            addition = min(bound - given[i], max(1, budget * loads[i] // mass), rest)
            given[i] = given[i] + addition
            rest = rest - addition
    return np.array(given)


def scatter_about(stream_key, dims, deviation, limit, cuts=(), kind=jnp.bfloat16):
    loudness = block_levels(stream_key, dims, cuts, -0.22, 0.18) if cuts else 1.0
    drawn = jax.random.normal(stream_key, dims, jnp.float32) * deviation * loudness
    return jnp.minimum(jnp.maximum(drawn, -limit), limit).astype(kind)


def setup_inputs(seed: int = 0) -> dict:
    splits = jax.random.split(jax.random.key(seed), 9)
    rhs = draw_rhs(jax.random.fold_in(splits[8], 71), 0)
    tile_weights = scatter_about(splits[1], (NTILES, TB, NB), (6 * TB) ** -0.5, 0.3125, ((0, 32),))
    tile_owner_keys = jax.random.split(jax.random.fold_in(splits[2], 1), NTILES // TILE_DEV)
    tile_owner_turns = jax.random.permutation(jax.random.fold_in(splits[2], 3), NTILES // TILE_DEV)
    tile_owner = jax.vmap(lambda own, number: routed_block(jax.random.fold_in(splits[2], 2), own, number, TILE_DEV, DEVICES, 1, CAP, 2))(tile_owner_keys, tile_owner_turns).reshape((NTILES, 1))
    tile_row = touch_ends(jax.random.randint(splits[3], (NTILES,), 0, BLK_DEV), jax.random.fold_in(splits[3], 1), 0, BLK_DEV - 1).astype(jnp.int32)
    axis_a = draw_axis_a(jax.random.fold_in(splits[8], 71), 0)
    axis_b = draw_axis_b(jax.random.fold_in(splits[8], 71), 0)
    coupling = draw_coupling(jax.random.fold_in(splits[8], 71), 0)
    noise = jnp.clip(jnp.exp(jax.random.uniform(splits[7], (R,), jnp.float32, math.log(0.1), math.log(1.0))), 0.1, 1.0)
    return {"rhs": rhs, "tile_weights": tile_weights, "tile_owner": tile_owner, "tile_row": tile_row, "axis_a": axis_a, "axis_b": axis_b, "coupling": coupling, "noise": noise}


def axis_pass(field, axis_a, axis_b):
    first = jnp.einsum('alrb,lbc->alrc', field.astype(jnp.float32), axis_b.astype(jnp.float32)).astype(jnp.bfloat16)
    return jnp.einsum('xla,alrc->xlrc', axis_a.astype(jnp.float32), first.astype(jnp.float32)).astype(jnp.bfloat16)


def reference(rhs, tile_weights, tile_owner, tile_row, axis_a, axis_b, coupling, noise):
    tile_count = tile_weights.shape[0]
    a_share = NA // N_OBS
    lvl_share = LEVELS // N_LVL
    owner = tile_owner[:, 0]
    a_index = (owner // N_LVL) * a_share + tile_row // lvl_share
    l_index = (owner % N_LVL) * lvl_share + tile_row % lvl_share
    flat = (a_index * LEVELS + l_index).astype(jnp.int32)
    block = math.gcd(tile_count, 1024)
    steps_count = tile_count // block
    weight_blocks = tile_weights.reshape(steps_count, block, TB, NB)
    flat_blocks = flat.reshape(steps_count, block)

    def operator(direction):
        low = direction.astype(jnp.bfloat16).reshape(R, tile_count, TB)
        low_tiles = jnp.transpose(low, (1, 0, 2)).reshape(steps_count, block, R, TB)

        def forward(total, pieces):
            values, weights, places = pieces
            part = jnp.einsum('krt,ktn->krn', values.astype(jnp.float32), weights.astype(jnp.float32)).astype(jnp.bfloat16)
            return total + jax.ops.segment_sum(part.astype(jnp.float32), places, num_segments=NA * LEVELS), None

        start = jnp.zeros((NA * LEVELS, R, NB), jnp.float32)
        node_sums, unused = lax.scan(forward, start, (low_tiles, weight_blocks, flat_blocks))
        node_sums = node_sums.astype(jnp.bfloat16).reshape(NA, LEVELS, R, NB)
        spread = axis_pass(node_sums, axis_a, axis_b)
        mixed = jnp.einsum('lm,amrc->alrc', coupling, spread.astype(jnp.float32), precision=lax.Precision.HIGHEST).astype(jnp.bfloat16)
        grid_values = axis_pass(mixed, axis_a, axis_b).reshape(NA * LEVELS, R, NB)

        def backward(carry, pieces):
            weights, places = pieces
            picked = grid_values[places].astype(jnp.float32)
            back = jnp.einsum('krn,ktn->krt', picked, weights.astype(jnp.float32)).astype(jnp.bfloat16)
            return carry, back

        unused, backs = lax.scan(backward, jnp.zeros((), jnp.float32), (weight_blocks, flat_blocks))
        backs = backs.reshape(tile_count, R, TB)
        back = jnp.transpose(backs, (1, 0, 2)).reshape(R, tile_count * TB)
        return back.astype(jnp.float32) + noise[:, None] * direction

    solution = jnp.zeros_like(rhs)
    residual = rhs
    direction = rhs
    norm_now = jnp.sum(residual * residual, axis=1)
    for step in range(ITERS):
        image = operator(direction)
        alpha = norm_now / jnp.sum(direction * image, axis=1)
        solution = solution + alpha[:, None] * direction
        residual = residual - alpha[:, None] * image
        if step + 1 < ITERS:
            norm_next = jnp.sum(residual * residual, axis=1)
            direction = residual + (norm_next / norm_now)[:, None] * direction
            norm_now = norm_next
    return solution, residual
```

```python
import jax
import jax.numpy as jnp
from jax import lax
from jax.experimental import pallas as pl
from jax.experimental.pallas import tpu as pltpu
from jax.sharding import Mesh
from jax.sharding import PartitionSpec as P


SPLIT = ("half", "part", "lvl")
PEERS = ("part", "lvl")
F32 = jnp.float32
BF16 = jnp.bfloat16
EXTRA = 16
BLOCK = 16
SCALARS = 8
UNROLL = 8
BASE = 128


def pieces(value):
    high = value.astype(BF16).astype(F32)
    rest = value - high
    middle = rest.astype(BF16).astype(F32)
    return high, middle, rest - middle


def pair_weights(weights_ref, k):
    pair = weights_ref[pl.ds(2 * k, 2)]
    zero = jnp.zeros_like(pair[0])
    return jnp.concatenate(
        [jnp.concatenate([pair[0], zero], 1), jnp.concatenate([zero, pair[1]], 1)], 0
    )


class Plan:
    def __init__(self, devices, columns, tiles, tile_obs, nodes, extra):
        self.devices, self.columns, self.tiles = devices, columns, tiles
        self.tile_obs, self.nodes = tile_obs, nodes
        self.mine = columns // devices
        self.data = self.mine * tiles
        self.rows = self.data + extra

    def rows_of(self, first):
        return pl.ds(first, self.devices, stride=self.rows)


def put_parts(plan, scratch, low, weights2, k):
    part = jnp.dot(low, weights2, preferred_element_type=F32)
    for c in range(plan.mine):
        rows = part[c * plan.devices : (c + 1) * plan.devices]
        for h in range(2):
            scratch[plan.rows_of(c * plan.tiles + 2 * k + h), :] = rows[
                :, h * plan.nodes : (h + 1) * plan.nodes
            ]


def put_sums(plan, scratch, sums):
    row = plan.data
    for value in sums:
        total = jnp.sum(value, axis=1, keepdims=True)
        total = jnp.broadcast_to(total, (plan.columns, plan.nodes))
        for c in range(plan.mine):
            for piece in pieces(total[c * plan.devices : (c + 1) * plan.devices]):
                scratch[plan.rows_of(row), :] = piece
                row += 1
    while row < plan.data + EXTRA:
        scratch[plan.rows_of(row), :] = jnp.zeros((plan.devices, plan.nodes), F32)
        row += 1


def write_out(plan, scratch, out_ref, setup=()):
    live = plan.data + EXTRA

    def cast(d, unused):
        rows = pl.ds(pl.multiple_of(d * plan.rows, 8), live)
        out_ref[d, :live] = scratch[rows, :].astype(BF16)
        row = live
        for block in setup:
            out_ref[d, row : row + block.shape[0]] = block
            row += block.shape[0]
        return unused

    lax.fori_loop(0, plan.devices, cast, 0, unroll=2)


def send_kernel(plan, low_ref, weights_ref, *refs):
    block = 2 * plan.tile_obs
    *setup_refs, out_ref, scratch = refs

    def step(k, total):
        field = low_ref[:, pl.ds(pl.multiple_of(k * block, block), block)]
        put_parts(plan, scratch, field.astype(BF16), pair_weights(weights_ref, k), k)
        return total + field * field

    total = lax.fori_loop(
        0, plan.tiles // 2, step, jnp.zeros((plan.columns, block), F32), unroll=UNROLL
    )
    put_sums(plan, scratch, [total])
    write_out(plan, scratch, out_ref, [ref[...] for ref in setup_refs])


def joined(plan, received_ref, source):
    return jnp.concatenate(
        [received_ref[source, c * plan.tiles : (c + 1) * plan.tiles] for c in range(plan.mine)], 1
    )


def owner_sum(plan, received_ref, first):
    sums = jnp.sum(received_ref[:, plan.data : plan.data + EXTRA].astype(F32), axis=0)
    return [
        sums[first + 3 * c : first + 3 * c + 1]
        + sums[first + 3 * c + 1 : first + 3 * c + 2]
        + sums[first + 3 * c + 2 : first + 3 * c + 3]
        for c in range(plan.mine)
    ]


def collect(plan, received_ref, index_ref, acc_ref):
    node_count = acc_ref.shape[0]
    acc_ref[...] = jnp.zeros_like(acc_ref)

    def step(j, unused):
        hots = []
        for h in range(2):
            index = index_ref[pl.ds(2 * j + h, 1), :]
            nodes = lax.broadcasted_iota(jnp.int32, (node_count, plan.tiles), 0)
            hots.append(jnp.where(nodes == index, 1.0, 0.0).astype(BF16))
        data = jnp.concatenate([joined(plan, received_ref, 2 * j + h) for h in range(2)], 0)
        acc_ref[...] += jnp.dot(jnp.concatenate(hots, 1), data, preferred_element_type=F32)
        return unused

    lax.fori_loop(0, plan.devices // 2, step, 0)


def grid_steps(plan, levels, sums_ref, axis_a_ref, axis_b_ref, coupling_ref, spread_ref, grid_ref):
    first = axis_a_ref.shape[1]

    def axes(field, l):
        steps = jnp.concatenate(
            [
                jnp.dot(
                    field[:, c * plan.nodes : (c + 1) * plan.nodes],
                    axis_b_ref[l],
                    preferred_element_type=F32,
                ).astype(BF16)
                for c in range(plan.mine)
            ],
            1,
        )
        return jnp.dot(axis_a_ref[l], steps, preferred_element_type=F32)

    for l in range(levels):
        field = sums_ref[l * first : (l + 1) * first]
        spread_ref[l] = axes(field, l).astype(BF16).astype(F32)
    for l in range(levels):
        mixed = coupling_ref[l, 0] * spread_ref[0]
        for m in range(1, levels):
            mixed = mixed + coupling_ref[l, m] * spread_ref[m]
        grid_ref[l * first : (l + 1) * first] = axes(mixed.astype(BF16), l).astype(BF16)


def products(plan, sums_ref, grid_ref):
    total = jnp.sum(sums_ref[...].astype(F32) * grid_ref[...].astype(F32), axis=0, keepdims=True)
    return [
        jnp.sum(total[:, c * plan.nodes : (c + 1) * plan.nodes], axis=1, keepdims=True)
        for c in range(plan.mine)
    ]


def give_back(plan, grid_ref, index_t_ref, out_ref, scalars):
    node_count = grid_ref.shape[0]
    group = 4

    rows = []
    for value in scalars:
        rows += list(pieces(jnp.broadcast_to(value, (1, plan.nodes))))
    rows.append(jnp.zeros((EXTRA - len(rows), plan.nodes), F32))
    extra = jnp.concatenate(rows, 0).astype(BF16)
    for j in range(plan.devices // group):
        hots = []
        for h in range(group):
            index = index_t_ref[:, j * group + h : j * group + h + 1]
            nodes = lax.broadcasted_iota(jnp.int32, (plan.tiles, node_count), 1)
            hots.append(jnp.where(nodes == index, 1.0, 0.0).astype(BF16))
        picked = jnp.dot(
            jnp.concatenate(hots, 0), grid_ref[...], preferred_element_type=F32
        ).astype(BF16)
        for h in range(group):
            for c in range(plan.mine):
                out_ref[j * group + h, c * plan.tiles : (c + 1) * plan.tiles] = picked[
                    h * plan.tiles : (h + 1) * plan.tiles, c * plan.nodes : (c + 1) * plan.nodes
                ]
            out_ref[j * group + h, plan.data : plan.data + EXTRA] = extra


def read_setup(
    plan, part, lvl, a_rows, lvl_here, b_rows, received_ref, axis_a_ref, axis_b_ref, index_ref,
    index_t_ref,
):
    base = plan.data + EXTRA
    for o in range(part):
        for v in range(lvl):
            for l in range(lvl_here):
                row = base + l * a_rows
                axis_a_ref[v * lvl_here + l, o * a_rows : (o + 1) * a_rows] = received_ref[
                    o * lvl + v, row : row + a_rows
                ]
                row = base + lvl_here * a_rows + l * b_rows
                axis_b_ref[v * lvl_here + l, o * b_rows : (o + 1) * b_rows] = received_ref[
                    o * lvl + v, row : row + b_rows
                ]
    row = base + lvl_here * (a_rows + b_rows)
    for d in range(plan.devices):
        split = received_ref[d, row : row + 8].astype(F32)
        index_ref[d : d + 1] = (split[0:1] * float(BASE) + split[1:2]).astype(jnp.int32)
    square = index_ref[...].astype(F32)
    square = jnp.concatenate(
        [square] + [jnp.zeros((plan.tiles - plan.devices, plan.tiles), F32)], 0
    )
    index_t_ref[...] = square.T.astype(jnp.int32)


def collect_kernel(plan, quantities, received_ref, index_ref, out_ref, acc_ref):
    collect(plan, received_ref, index_ref, acc_ref)
    node_count = acc_ref.shape[0]
    out_ref[:node_count] = acc_ref[...].astype(BF16)
    rows = []
    for q in range(quantities):
        sums = owner_sum(plan, received_ref, 3 * plan.mine * q)
        rows += list(pieces(jnp.concatenate(sums, 1)))
    rows.append(jnp.zeros((SCALARS - len(rows), plan.mine * plan.nodes), F32))
    out_ref[node_count:] = jnp.concatenate(rows, 0).astype(BF16)


def grid_kernel(
    plan, opening, start_column, coupling_ref, noise_ref, place_ref, own_ref, other_ref, own_a_ref,
    other_a_ref, axis_b_ref, index_t_ref, *refs,
):
    axis_a_ref, sums_ref, grid_ref, spread_ref = refs[-4:]
    node_count, _ = sums_ref.shape
    half = own_a_ref.shape[1]
    axis_a_ref[:, pl.ds(pl.multiple_of(place_ref[1] * half, half), half)] = own_a_ref[...]
    axis_a_ref[:, pl.ds(pl.multiple_of((1 - place_ref[1]) * half, half), half)] = other_a_ref[...]

    total = own_ref[:node_count].astype(F32) + other_ref[:node_count].astype(F32)
    rows = own_ref[node_count:].astype(F32) + other_ref[node_count:].astype(F32)
    square = rows[0:1] + rows[1:2] + rows[2:3]
    if opening:
        out_ref, kept_ref, square_ref = refs[:3]
        kept_ref[...] = total
        square_ref[...] = square
        length, beta = square, None
    else:
        kept_ref, square_ref, out_ref = refs[:3]
        cross = rows[3:4] + rows[4:5] + rows[5:6]
        old = square_ref[...]
        beta = square / old
        total = total + beta * kept_ref[...]
        length = square + beta * (2.0 * cross + beta * old)
    sums_ref[...] = total.astype(BF16)
    levels = axis_a_ref.shape[0]
    grid_steps(plan, levels, sums_ref, axis_a_ref, axis_b_ref, coupling_ref, spread_ref, grid_ref)
    quads = products(plan, sums_ref, grid_ref)
    alphas, betas = [], []
    for c in range(plan.mine):
        here = slice(c * plan.nodes, (c + 1) * plan.nodes)
        noise = noise_ref[start_column + c * plan.devices + place_ref[0]]
        alphas.append(square[:, here] / (quads[c] + noise * length[:, here]))
        if beta is not None:
            betas.append(beta[:, here])
    give_back(plan, grid_ref, index_t_ref, out_ref, alphas + betas)


def unpack(plan, received_ref, scratch):
    def cast(d, unused):
        scratch[pl.ds(pl.multiple_of(d * plan.rows, 8), plan.rows), :] = received_ref[d].astype(F32)
        return unused

    lax.fori_loop(0, plan.devices, cast, 0, unroll=2)


def scalar_of(plan, scratch, first):
    parts = []
    for c in range(plan.mine):
        row = plan.data + first + 3 * c
        parts.append(
            scratch[plan.rows_of(row), :]
            + scratch[plan.rows_of(row + 1), :]
            + scratch[plan.rows_of(row + 2), :]
        )
    return jnp.concatenate(parts, 0)


def tile_values(plan, scratch, weights2, k):
    halves = []
    for h in range(2):
        halves.append(
            jnp.concatenate(
                [
                    scratch[plan.rows_of(c * plan.tiles + 2 * k + h), :].astype(BF16)
                    for c in range(plan.mine)
                ],
                0,
            )
        )
    return lax.dot_general(
        jnp.concatenate(halves, 1), weights2, (((1,), (1,)), ((), ())),
        preferred_element_type=F32,
    )


def turn_kernel(
    plan, received_ref, rhs_ref, weights_ref, noise_ref, residual_ref, alpha_ref, out_ref, scratch,
    out_scratch,
):
    block = 2 * plan.tile_obs
    unpack(plan, received_ref, scratch)
    alpha = scalar_of(plan, scratch, 0)
    alpha_ref[...] = alpha
    alpha = alpha[:, :block]
    noise = jnp.broadcast_to(noise_ref[...], (plan.columns, block))

    def step(k, totals):
        here = pl.ds(pl.multiple_of(k * block, block), block)
        weights2 = pair_weights(weights_ref, k)
        old = rhs_ref[:, here]
        image = tile_values(plan, scratch, weights2, k) + noise * old
        residual = old - alpha * image
        residual_ref[:, here] = residual
        put_parts(plan, out_scratch, residual.astype(BF16), weights2, k)
        return totals[0] + residual * residual, totals[1] + residual * old

    zero = jnp.zeros((plan.columns, block), F32)
    totals = lax.fori_loop(0, plan.tiles // 2, step, (zero, zero), unroll=UNROLL)
    put_sums(plan, out_scratch, totals)
    write_out(plan, out_scratch, out_ref)


def last_kernel(
    plan, received_ref, rhs_ref, weights_ref, noise_ref, old_residual_ref, alpha_ref, *refs
):
    solution_ref, residual_ref, scratch = refs[-3:]
    block = 2 * plan.tile_obs
    unpack(plan, received_ref, scratch)
    alpha = scalar_of(plan, scratch, 0)[:, :block]
    beta = scalar_of(plan, scratch, 3 * plan.mine)[:, :block]
    first_alpha = alpha_ref[:, :block]
    noise = jnp.broadcast_to(noise_ref[...], (plan.columns, block))

    def step(k, unused):
        here = pl.ds(pl.multiple_of(k * block, block), block)
        rhs = rhs_ref[:, here]
        old = old_residual_ref[:, here]
        direction = old + beta * rhs
        image = tile_values(plan, scratch, pair_weights(weights_ref, k), k) + noise * direction
        solution_ref[:, here] = first_alpha * rhs + alpha * direction
        residual_ref[:, here] = old - alpha * image
        return unused

    lax.fori_loop(0, plan.tiles // 2, step, 0, unroll=UNROLL)


VMEM = pl.BlockSpec(memory_space=pltpu.VMEM)
SMEM = pl.BlockSpec(memory_space=pltpu.SMEM)
ANY = pl.BlockSpec(memory_space=pl.ANY)


def by_columns(rhs, tile_weights, tile_owner, tile_row, axis_a, axis_b, coupling, noise):
    peers = lax.axis_size(PEERS)
    part, lvl = lax.axis_size("part"), lax.axis_size("lvl")
    tiles, tile_obs, nodes = tile_weights.shape
    all_columns, width = rhs.shape
    groups = 2 if all_columns % (2 * peers) == 0 else 1
    columns = all_columns // groups
    a_rows, lvl_here, first_axis = axis_a.shape
    b_rows = nodes // part
    levels = lvl * lvl_here
    node_count = levels * first_axis
    place = jnp.stack([lax.axis_index(PEERS), lax.axis_index("half")]).astype(jnp.int32)
    setup_rows = lvl_here * (a_rows + b_rows) + BLOCK
    start = Plan(peers, columns, tiles, tile_obs, nodes, EXTRA + setup_rows)
    plan = Plan(peers, columns, tiles, tile_obs, nodes, EXTRA)
    grid_width = plan.mine * nodes

    owner = tile_owner[:, 0]
    first = owner // lvl * a_rows + tile_row // lvl_here
    target = (owner % lvl * lvl_here + tile_row % lvl_here) * first_axis + first
    index = jnp.stack([target // BASE, target % BASE]).astype(BF16)
    my_b = lax.dynamic_slice_in_dim(axis_b, lax.axis_index("part") * b_rows, b_rows, 1)
    setup = (
        jnp.transpose(axis_a, (1, 0, 2)).reshape(lvl_here * a_rows, first_axis),
        my_b.reshape(lvl_here * b_rows, nodes),
        jnp.concatenate([index, jnp.zeros((BLOCK - 2, tiles), BF16)], 0),
    )

    def exchange(field):
        return lax.all_to_all(field, PEERS, split_axis=0, concat_axis=0, tiled=True)

    def swap(field):
        return lax.ppermute(field, "half", [(0, 1), (1, 0)])

    def shape(*dims, dtype=F32):
        return jax.ShapeDtypeStruct(dims, dtype)

    def part_of(g, *dims):
        return pl.BlockSpec(dims, lambda i: (g,) + (0,) * (len(dims) - 1), memory_space=pltpu.VMEM)

    noise_column = noise[:, None]
    parts_scratch = [pltpu.VMEM((peers * plan.rows, nodes), F32)]
    grid_scratch = [
        pltpu.VMEM((levels, first_axis, first_axis), BF16),
        pltpu.VMEM((node_count, grid_width), BF16),
        pltpu.VMEM((node_count, grid_width), BF16),
        pltpu.VMEM((levels, first_axis, grid_width), F32),
    ]
    sent_shape = shape(peers, plan.rows, nodes, dtype=BF16)
    residual_shape = shape(columns, width)

    def send(g):
        here = start if g == 0 else plan
        return pl.pallas_call(
            lambda *refs: send_kernel(here, *refs),
            out_shape=shape(peers, here.rows, nodes, dtype=BF16),
            in_specs=[part_of(g, columns, width), VMEM] + [VMEM] * 3 * (g == 0),
            out_specs=VMEM,
            scratch_shapes=[pltpu.VMEM((peers * here.rows, nodes), F32)],
            grid=(1,),
        )(rhs, tile_weights, *(setup if g == 0 else ()))

    def read(received):
        return pl.pallas_call(
            lambda *refs: read_setup(start, part, lvl, a_rows, lvl_here, b_rows, *refs),
            out_shape=(
                shape(levels, first_axis // 2, first_axis, dtype=BF16),
                shape(levels, nodes, nodes, dtype=BF16),
                shape(peers, tiles, dtype=jnp.int32),
                shape(tiles, tiles, dtype=jnp.int32),
            ),
            in_specs=[VMEM],
            out_specs=[VMEM] * 4,
            name="read_setup",
        )(received)

    def collected(here, quantities, received, index):
        return pl.pallas_call(
            lambda *refs: collect_kernel(here, quantities, *refs),
            out_shape=shape(node_count + SCALARS, grid_width, dtype=BF16),
            in_specs=[VMEM] * 2,
            out_specs=VMEM,
            scratch_shapes=[pltpu.VMEM((node_count, grid_width), F32)],
        )(received, index)

    def grid(g, own, other, tables, kept):
        keep = (shape(node_count, grid_width), shape(1, grid_width)) if not kept else ()
        return pl.pallas_call(
            lambda *refs: grid_kernel(plan, not kept, g * columns, *refs),
            out_shape=(sent_shape,) + keep,
            in_specs=[SMEM] * 3 + [VMEM] * (6 + len(kept)),
            out_specs=[VMEM] * (1 + len(keep)),
            scratch_shapes=grid_scratch,
        )(coupling, noise, place, own, other, *tables, *kept)

    def turn(g, received):
        return pl.pallas_call(
            lambda *refs: turn_kernel(plan, *refs),
            out_shape=(residual_shape, shape(columns, nodes), sent_shape),
            in_specs=[VMEM, part_of(g, columns, width), VMEM, part_of(g, columns, 1)],
            out_specs=[VMEM] * 3,
            scratch_shapes=parts_scratch * 2,
            grid=(1,),
        )(received, rhs, tile_weights, noise_column)

    def last(g, received, residual, alpha, outputs):
        return pl.pallas_call(
            lambda *refs: last_kernel(plan, *refs),
            out_shape=(shape(*rhs.shape), shape(*rhs.shape)),
            in_specs=[VMEM, part_of(g, columns, width), VMEM, part_of(g, columns, 1), VMEM, VMEM]
            + [ANY] * len(outputs),
            out_specs=[part_of(g, columns, width)] * 2,
            input_output_aliases={6 + i: i for i in range(len(outputs))},
            scratch_shapes=parts_scratch,
            grid=(1,),
        )(received, rhs, tile_weights, noise_column, residual, alpha, *outputs)

    each = range(groups)
    received = [exchange(send(g)) for g in each]
    own_a, full_b, index, index_t = read(received[0])
    other_a = swap(own_a)
    tables = (own_a, other_a, full_b, index_t)
    own = [collected(start if g == 0 else plan, 1, received[g], index) for g in each]
    other = [swap(own[g]) for g in each]
    grids = [grid(g, own[g], other[g], tables, ()) for g in each]
    received = [exchange(grids[g][0]) for g in each]
    turned = [turn(g, received[g]) for g in each]
    received = [exchange(turned[g][2]) for g in each]
    own = [collected(plan, 2, received[g], index) for g in each]
    other = [swap(own[g]) for g in each]
    sent = [grid(g, own[g], other[g], tables, grids[g][1:])[0] for g in each]
    received = [exchange(sent[g]) for g in each]
    outputs = ()
    for g in each:
        outputs = last(g, received[g], turned[g][0], turned[g][1], outputs)
    return outputs


def solution(mesh):
    obs, lvl = mesh.shape["obs"], mesh.shape["lvl"]
    split = Mesh(mesh.devices.reshape(2, obs // 2, lvl), SPLIT)
    in_specs = (
        P(None, SPLIT),
        P(SPLIT, None, None),
        P(SPLIT, None),
        P(SPLIT),
        P(("half", "part"), "lvl", None),
        P("lvl", None, None),
        P(),
        P(),
    )
    out_specs = (P(None, SPLIT), P(None, SPLIT))
    return jax.shard_map(
        by_columns, mesh=split, in_specs=in_specs, out_specs=out_specs, check_vma=False
    )
```

```python
import jax
import jax.numpy as jnp
from jax import lax
from jax.experimental import pallas as pl
from jax.experimental.pallas import tpu as pltpu
from jax.sharding import Mesh
from jax.sharding import PartitionSpec as P


SPLIT = ("half", "part", "lvl")
PEERS = ("part", "lvl")
F32 = jnp.float32
BF16 = jnp.bfloat16
EXTRA = 16
BLOCK = 16
SCALARS = 8
UNROLL = 8
VMEM_LIMIT = 28 * 1024 * 1024
BASE = 128


def pieces(value):
    high = value.astype(BF16).astype(F32)
    rest = value - high
    middle = rest.astype(BF16).astype(F32)
    return high, middle, rest - middle


def pair_weights(weights_ref, k):
    pair = weights_ref[pl.ds(2 * k, 2)]
    zero = jnp.zeros_like(pair[0])
    return jnp.concatenate(
        [jnp.concatenate([pair[0], zero], 1), jnp.concatenate([zero, pair[1]], 1)], 0
    )


class Plan:
    def __init__(self, devices, columns, tiles, tile_obs, nodes, extra):
        self.devices, self.columns, self.tiles = devices, columns, tiles
        self.tile_obs, self.nodes = tile_obs, nodes
        self.mine = columns // devices
        self.data = self.mine * tiles
        self.rows = self.data + extra

    def rows_of(self, first):
        return pl.ds(first, self.devices, stride=self.rows)


def put_parts(plan, scratch, low, weights2, k):
    part = jnp.dot(low, weights2, preferred_element_type=F32)
    for c in range(plan.mine):
        rows = part[c * plan.devices : (c + 1) * plan.devices]
        for h in range(2):
            scratch[plan.rows_of(c * plan.tiles + 2 * k + h), :] = rows[
                :, h * plan.nodes : (h + 1) * plan.nodes
            ]


def put_sums(plan, scratch, sums):
    row = plan.data
    for value in sums:
        total = jnp.sum(value, axis=1, keepdims=True)
        total = jnp.broadcast_to(total, (plan.columns, plan.nodes))
        for c in range(plan.mine):
            for piece in pieces(total[c * plan.devices : (c + 1) * plan.devices]):
                scratch[plan.rows_of(row), :] = piece
                row += 1
    while row < plan.data + EXTRA:
        scratch[plan.rows_of(row), :] = jnp.zeros((plan.devices, plan.nodes), F32)
        row += 1


def write_out(plan, scratch, out_ref, setup=()):
    live = plan.data + EXTRA

    def cast(d, unused):
        rows = pl.ds(pl.multiple_of(d * plan.rows, 8), live)
        out_ref[d, :live] = scratch[rows, :].astype(BF16)
        row = live
        for block in setup:
            out_ref[d, row : row + block.shape[0]] = block
            row += block.shape[0]
        return unused

    lax.fori_loop(0, plan.devices, cast, 0, unroll=2)


def send_kernel(plan, low_ref, weights_ref, *refs):
    block = 2 * plan.tile_obs
    *setup_refs, out_ref, scratch = refs

    def step(k, total):
        field = low_ref[:, pl.ds(pl.multiple_of(k * block, block), block)]
        put_parts(plan, scratch, field.astype(BF16), pair_weights(weights_ref, k), k)
        return total + field * field

    total = lax.fori_loop(
        0, plan.tiles // 2, step, jnp.zeros((plan.columns, block), F32), unroll=UNROLL
    )
    put_sums(plan, scratch, [total])
    write_out(plan, scratch, out_ref, [ref[...] for ref in setup_refs])


def joined(plan, received_ref, source):
    return jnp.concatenate(
        [received_ref[source, c * plan.tiles : (c + 1) * plan.tiles] for c in range(plan.mine)], 1
    )


def owner_sum(plan, received_ref, first):
    sums = jnp.sum(received_ref[:, plan.data : plan.data + EXTRA].astype(F32), axis=0)
    return [
        sums[first + 3 * c : first + 3 * c + 1]
        + sums[first + 3 * c + 1 : first + 3 * c + 2]
        + sums[first + 3 * c + 2 : first + 3 * c + 3]
        for c in range(plan.mine)
    ]


def collect(plan, received_ref, index_ref, acc_ref):
    node_count = acc_ref.shape[0]
    acc_ref[...] = jnp.zeros_like(acc_ref)

    def step(j, unused):
        hots = []
        for h in range(2):
            index = index_ref[pl.ds(2 * j + h, 1), :]
            nodes = lax.broadcasted_iota(jnp.int32, (node_count, plan.tiles), 0)
            hots.append(jnp.where(nodes == index, 1.0, 0.0).astype(BF16))
        data = jnp.concatenate([joined(plan, received_ref, 2 * j + h) for h in range(2)], 0)
        acc_ref[...] += jnp.dot(jnp.concatenate(hots, 1), data, preferred_element_type=F32)
        return unused

    lax.fori_loop(0, plan.devices // 2, step, 0)


def grid_steps(plan, levels, sums_ref, axis_a_ref, axis_b_ref, coupling_ref, spread_ref, grid_ref):
    first = axis_a_ref.shape[1]

    def axes(field, l):
        steps = jnp.concatenate(
            [
                jnp.dot(
                    field[:, c * plan.nodes : (c + 1) * plan.nodes],
                    axis_b_ref[l],
                    preferred_element_type=F32,
                ).astype(BF16)
                for c in range(plan.mine)
            ],
            1,
        )
        return jnp.dot(axis_a_ref[l], steps, preferred_element_type=F32)

    for l in range(levels):
        field = sums_ref[l * first : (l + 1) * first]
        spread_ref[l] = axes(field, l).astype(BF16).astype(F32)
    for l in range(levels):
        mixed = coupling_ref[l, 0] * spread_ref[0]
        for m in range(1, levels):
            mixed = mixed + coupling_ref[l, m] * spread_ref[m]
        grid_ref[l * first : (l + 1) * first] = axes(mixed.astype(BF16), l).astype(BF16)


def products(plan, sums_ref, grid_ref):
    total = jnp.sum(sums_ref[...].astype(F32) * grid_ref[...].astype(F32), axis=0, keepdims=True)
    return [
        jnp.sum(total[:, c * plan.nodes : (c + 1) * plan.nodes], axis=1, keepdims=True)
        for c in range(plan.mine)
    ]


def give_back(plan, grid_ref, index_t_ref, out_ref, scalars):
    node_count = grid_ref.shape[0]
    group = 4

    rows = []
    for value in scalars:
        rows += list(pieces(jnp.broadcast_to(value, (1, plan.nodes))))
    rows.append(jnp.zeros((EXTRA - len(rows), plan.nodes), F32))
    extra = jnp.concatenate(rows, 0).astype(BF16)
    for j in range(plan.devices // group):
        hots = []
        for h in range(group):
            index = index_t_ref[:, j * group + h : j * group + h + 1]
            nodes = lax.broadcasted_iota(jnp.int32, (plan.tiles, node_count), 1)
            hots.append(jnp.where(nodes == index, 1.0, 0.0).astype(BF16))
        picked = jnp.dot(
            jnp.concatenate(hots, 0), grid_ref[...], preferred_element_type=F32
        ).astype(BF16)
        for h in range(group):
            for c in range(plan.mine):
                out_ref[j * group + h, c * plan.tiles : (c + 1) * plan.tiles] = picked[
                    h * plan.tiles : (h + 1) * plan.tiles, c * plan.nodes : (c + 1) * plan.nodes
                ]
            out_ref[j * group + h, plan.data : plan.data + EXTRA] = extra


def read_index(plan, base, received_ref, index_ref, index_t_ref):
    for d in range(plan.devices):
        split = received_ref[d, base : base + 8].astype(F32)
        index_ref[d : d + 1] = (split[0:1] * float(BASE) + split[1:2]).astype(jnp.int32)
    square = index_ref[...].astype(F32)
    square = jnp.concatenate(
        [square] + [jnp.zeros((plan.tiles - plan.devices, plan.tiles), F32)], 0
    )
    index_t_ref[...] = square.T.astype(jnp.int32)


def read_axes(plan, base, lvl, received_ref, own_a_ref, other_a_ref):
    part = plan.devices // lvl
    lvl_here = own_a_ref.shape[0] // lvl
    for o in range(part):
        for v in range(lvl):
            row = base
            for table_ref in (own_a_ref, other_a_ref):
                count = table_ref.shape[1] // part
                for l in range(lvl_here):
                    table_ref[v * lvl_here + l, o * count : (o + 1) * count] = received_ref[
                        o * lvl + v, row : row + count
                    ]
                    row += count


def collect_kernel(plan, quantities, received_ref, index_ref, out_ref, acc_ref):
    collect(plan, received_ref, index_ref, acc_ref)
    node_count = acc_ref.shape[0]
    out_ref[:node_count] = acc_ref[...].astype(BF16)
    rows = []
    for q in range(quantities):
        sums = owner_sum(plan, received_ref, 3 * plan.mine * q)
        rows += list(pieces(jnp.concatenate(sums, 1)))
    rows.append(jnp.zeros((SCALARS - len(rows), plan.mine * plan.nodes), F32))
    out_ref[node_count:] = jnp.concatenate(rows, 0).astype(BF16)


def grid_kernel(
    plan, opening, lvl, start_column, coupling_ref, noise_ref, place_ref, own_ref, other_ref,
    own_a_ref, other_a_ref, index_t_ref, *refs,
):
    axis_a_ref, axis_b_ref, sums_ref, grid_ref, spread_ref = refs[-5:]
    b_refs, refs = refs[:lvl], refs[lvl:]
    lvl_here = axis_b_ref.shape[0] // lvl
    for k in range(lvl):
        source = (place_ref[2] + lvl - k) % lvl
        axis_b_ref[pl.ds(source * lvl_here, lvl_here)] = b_refs[k][...]
    node_count, _ = sums_ref.shape
    half = own_a_ref.shape[1]
    axis_a_ref[:, pl.ds(pl.multiple_of(place_ref[1] * half, half), half)] = own_a_ref[...]
    axis_a_ref[:, pl.ds(pl.multiple_of((1 - place_ref[1]) * half, half), half)] = other_a_ref[...]

    total = own_ref[:node_count].astype(F32) + other_ref[:node_count].astype(F32)
    rows = own_ref[node_count:].astype(F32) + other_ref[node_count:].astype(F32)
    square = rows[0:1] + rows[1:2] + rows[2:3]
    if opening:
        out_ref, kept_ref, square_ref = refs[:3]
        kept_ref[...] = total
        square_ref[...] = square
        length, beta = square, None
    else:
        kept_ref, square_ref, out_ref = refs[:3]
        cross = rows[3:4] + rows[4:5] + rows[5:6]
        old = square_ref[...]
        beta = square / old
        total = total + beta * kept_ref[...]
        length = square + beta * (2.0 * cross + beta * old)
    sums_ref[...] = total.astype(BF16)
    levels = axis_a_ref.shape[0]
    grid_steps(plan, levels, sums_ref, axis_a_ref, axis_b_ref, coupling_ref, spread_ref, grid_ref)
    quads = products(plan, sums_ref, grid_ref)
    alphas, betas = [], []
    for c in range(plan.mine):
        here = slice(c * plan.nodes, (c + 1) * plan.nodes)
        noise = noise_ref[start_column + c * plan.devices + place_ref[0]]
        alphas.append(square[:, here] / (quads[c] + noise * length[:, here]))
        if beta is not None:
            betas.append(beta[:, here])
    give_back(plan, grid_ref, index_t_ref, out_ref, alphas + betas)


def unpack(plan, received_ref, scratch):
    def cast(d, unused):
        scratch[pl.ds(pl.multiple_of(d * plan.rows, 8), plan.rows), :] = received_ref[d].astype(F32)
        return unused

    lax.fori_loop(0, plan.devices, cast, 0, unroll=2)


def scalar_of(plan, scratch, first):
    parts = []
    for c in range(plan.mine):
        row = plan.data + first + 3 * c
        parts.append(
            scratch[plan.rows_of(row), :]
            + scratch[plan.rows_of(row + 1), :]
            + scratch[plan.rows_of(row + 2), :]
        )
    return jnp.concatenate(parts, 0)


def tile_values(plan, scratch, weights2, k):
    halves = []
    for h in range(2):
        halves.append(
            jnp.concatenate(
                [
                    scratch[plan.rows_of(c * plan.tiles + 2 * k + h), :].astype(BF16)
                    for c in range(plan.mine)
                ],
                0,
            )
        )
    return lax.dot_general(
        jnp.concatenate(halves, 1), weights2, (((1,), (1,)), ((), ())),
        preferred_element_type=F32,
    )


def turn_kernel(
    plan, received_ref, rhs_ref, weights_ref, noise_ref, residual_ref, alpha_ref, out_ref, scratch,
    out_scratch,
):
    block = 2 * plan.tile_obs
    unpack(plan, received_ref, scratch)
    alpha = scalar_of(plan, scratch, 0)
    alpha_ref[...] = alpha
    alpha = alpha[:, :block]
    noise = jnp.broadcast_to(noise_ref[...], (plan.columns, block))

    def step(k, totals):
        here = pl.ds(pl.multiple_of(k * block, block), block)
        weights2 = pair_weights(weights_ref, k)
        old = rhs_ref[:, here]
        image = tile_values(plan, scratch, weights2, k) + noise * old
        residual = old - alpha * image
        residual_ref[:, here] = residual
        put_parts(plan, out_scratch, residual.astype(BF16), weights2, k)
        return totals[0] + residual * residual, totals[1] + residual * old

    zero = jnp.zeros((plan.columns, block), F32)
    totals = lax.fori_loop(0, plan.tiles // 2, step, (zero, zero), unroll=UNROLL)
    put_sums(plan, out_scratch, totals)
    write_out(plan, out_scratch, out_ref)


def last_kernel(
    plan, received_ref, rhs_ref, weights_ref, noise_ref, old_residual_ref, alpha_ref, *refs
):
    solution_ref, residual_ref, scratch = refs[-3:]
    block = 2 * plan.tile_obs
    unpack(plan, received_ref, scratch)
    alpha = scalar_of(plan, scratch, 0)[:, :block]
    beta = scalar_of(plan, scratch, 3 * plan.mine)[:, :block]
    first_alpha = alpha_ref[:, :block]
    noise = jnp.broadcast_to(noise_ref[...], (plan.columns, block))

    def step(k, unused):
        here = pl.ds(pl.multiple_of(k * block, block), block)
        rhs = rhs_ref[:, here]
        old = old_residual_ref[:, here]
        direction = old + beta * rhs
        image = tile_values(plan, scratch, pair_weights(weights_ref, k), k) + noise * direction
        solution_ref[:, here] = first_alpha * rhs + alpha * direction
        residual_ref[:, here] = old - alpha * image
        return unused

    lax.fori_loop(0, plan.tiles // 2, step, 0, unroll=UNROLL)


VMEM = pl.BlockSpec(memory_space=pltpu.VMEM)
SMEM = pl.BlockSpec(memory_space=pltpu.SMEM)
ANY = pl.BlockSpec(memory_space=pl.ANY)
PARAMS = pltpu.CompilerParams(vmem_limit_bytes=VMEM_LIMIT)


def by_columns(rhs, tile_weights, tile_owner, tile_row, axis_a, axis_b, coupling, noise):
    peers = lax.axis_size(PEERS)
    lvl = lax.axis_size("lvl")
    tiles, tile_obs, nodes = tile_weights.shape
    all_columns, width = rhs.shape
    groups = 2 if all_columns % (2 * peers) == 0 else 1
    columns = all_columns // groups
    a_rows, lvl_here, first_axis = axis_a.shape
    levels = lvl * lvl_here
    node_count = levels * first_axis
    place = jnp.stack(
        [lax.axis_index(PEERS), lax.axis_index("half"), lax.axis_index("lvl")]
    ).astype(jnp.int32)
    plan = Plan(peers, columns, tiles, tile_obs, nodes, EXTRA)
    grid_width = plan.mine * nodes

    owner = tile_owner[:, 0]
    first = owner // lvl * a_rows + tile_row // lvl_here
    target = (owner % lvl * lvl_here + tile_row % lvl_here) * first_axis + first
    index = jnp.stack([target // BASE, target % BASE]).astype(BF16)

    def exchange(field):
        return lax.all_to_all(field, PEERS, split_axis=0, concat_axis=0, tiled=True)

    def swap(field):
        return lax.ppermute(field, "half", [(0, 1), (1, 0)])

    my_a = jnp.transpose(axis_a, (1, 0, 2)).reshape(lvl_here * a_rows, first_axis)
    tables = [my_a, swap(my_a)]
    setups = [[] for _ in range(groups)]
    setups[0] += [jnp.concatenate([index, jnp.zeros((BLOCK - 2, tiles), BF16)], 0)]
    setups[-1] += tables
    starts = [
        Plan(peers, columns, tiles, tile_obs, nodes, EXTRA + sum(t.shape[0] for t in setup))
        for setup in setups
    ]
    tables_row = starts[-1].rows - sum(t.shape[0] for t in tables)

    def shape(*dims, dtype=F32):
        return jax.ShapeDtypeStruct(dims, dtype)

    def part_of(g, *dims):
        return pl.BlockSpec(dims, lambda i: (g,) + (0,) * (len(dims) - 1), memory_space=pltpu.VMEM)

    noise_column = noise[:, None]
    parts_scratch = [pltpu.VMEM((peers * plan.rows, nodes), F32)]
    grid_scratch = [
        pltpu.VMEM((levels, first_axis, first_axis), BF16),
        pltpu.VMEM((levels, nodes, nodes), BF16),
        pltpu.VMEM((node_count, grid_width), BF16),
        pltpu.VMEM((node_count, grid_width), BF16),
        pltpu.VMEM((levels, first_axis, grid_width), F32),
    ]
    sent_shape = shape(peers, plan.rows, nodes, dtype=BF16)
    residual_shape = shape(columns, width)

    def send(g):
        here = starts[g]
        return pl.pallas_call(
            lambda *refs: send_kernel(here, *refs),
            out_shape=shape(peers, here.rows, nodes, dtype=BF16),
            in_specs=[part_of(g, columns, width), VMEM] + [VMEM] * len(setups[g]),
            out_specs=VMEM,
            scratch_shapes=[pltpu.VMEM((peers * here.rows, nodes), F32)],
            grid=(1,),
            compiler_params=PARAMS,
        )(rhs, tile_weights, *setups[g])

    def find(received):
        return pl.pallas_call(
            lambda *refs: read_index(plan, plan.data + EXTRA, *refs),
            out_shape=(
                shape(peers, tiles, dtype=jnp.int32),
                shape(tiles, tiles, dtype=jnp.int32),
            ),
            in_specs=[VMEM],
            out_specs=[VMEM] * 2,
            compiler_params=PARAMS,
            name="read_index",
        )(received)

    def read(received):
        return pl.pallas_call(
            lambda *refs: read_axes(plan, tables_row, lvl, *refs),
            out_shape=(
                shape(levels, first_axis // 2, first_axis, dtype=BF16),
                shape(levels, first_axis // 2, first_axis, dtype=BF16),
            ),
            in_specs=[VMEM],
            out_specs=[VMEM] * 2,
            compiler_params=PARAMS,
            name="read_axes",
        )(received)

    def collected(here, quantities, received, index):
        return pl.pallas_call(
            lambda *refs: collect_kernel(here, quantities, *refs),
            out_shape=shape(node_count + SCALARS, grid_width, dtype=BF16),
            in_specs=[VMEM] * 2,
            out_specs=VMEM,
            scratch_shapes=[pltpu.VMEM((node_count, grid_width), F32)],
            compiler_params=PARAMS,
        )(received, index)

    def grid(g, own, other, tables, kept):
        keep = (shape(node_count, grid_width), shape(1, grid_width)) if not kept else ()
        return pl.pallas_call(
            lambda *refs: grid_kernel(plan, not kept, lvl, g * columns, *refs),
            out_shape=(sent_shape,) + keep,
            in_specs=[SMEM] * 3 + [VMEM] * (2 + len(tables) + len(kept)),
            out_specs=[VMEM] * (1 + len(keep)),
            scratch_shapes=grid_scratch,
            compiler_params=PARAMS,
        )(coupling, noise, place, own, other, *tables, *kept)

    def turn(g, received):
        return pl.pallas_call(
            lambda *refs: turn_kernel(plan, *refs),
            out_shape=(residual_shape, shape(columns, nodes), sent_shape),
            in_specs=[VMEM, part_of(g, columns, width), VMEM, part_of(g, columns, 1)],
            out_specs=[VMEM] * 3,
            scratch_shapes=parts_scratch * 2,
            grid=(1,),
            compiler_params=PARAMS,
        )(received, rhs, tile_weights, noise_column)

    def last(g, received, residual, alpha, outputs):
        return pl.pallas_call(
            lambda *refs: last_kernel(plan, *refs),
            out_shape=(shape(*rhs.shape), shape(*rhs.shape)),
            in_specs=[VMEM, part_of(g, columns, width), VMEM, part_of(g, columns, 1), VMEM, VMEM]
            + [ANY] * len(outputs),
            out_specs=[part_of(g, columns, width)] * 2,
            input_output_aliases={6 + i: i for i in range(len(outputs))},
            scratch_shapes=parts_scratch,
            grid=(1,),
            compiler_params=PARAMS,
        )(received, rhs, tile_weights, noise_column, residual, alpha, *outputs)

    each = range(groups)
    received = [exchange(send(g)) for g in each]
    all_b = [axis_b]
    for k in range(1, lvl):
        all_b.append(
            lax.ppermute(axis_b, "lvl", [(v, (v + k) % lvl) for v in range(lvl)])
        )
    index, index_t = find(received[0])
    tables = (*read(received[-1]), index_t, *all_b)
    own = [collected(starts[g], 1, received[g], index) for g in each]
    other = [swap(own[g]) for g in each]
    grids = [grid(g, own[g], other[g], tables, ()) for g in each]
    received = [exchange(grids[g][0]) for g in each]
    turned = [turn(g, received[g]) for g in each]
    received = [exchange(turned[g][2]) for g in each]
    own = [collected(plan, 2, received[g], index) for g in each]
    other = [swap(own[g]) for g in each]
    sent = [grid(g, own[g], other[g], tables, grids[g][1:])[0] for g in each]
    received = [exchange(sent[g]) for g in each]
    outputs = ()
    for g in each:
        outputs = last(g, received[g], turned[g][0], turned[g][1], outputs)
    return outputs


def solution(mesh):
    obs, lvl = mesh.shape["obs"], mesh.shape["lvl"]
    split = Mesh(mesh.devices.reshape(2, obs // 2, lvl), SPLIT)
    in_specs = (
        P(None, SPLIT),
        P(SPLIT, None, None),
        P(SPLIT, None),
        P(SPLIT),
        P(("half", "part"), "lvl", None),
        P("lvl", None, None),
        P(),
        P(),
    )
    out_specs = (P(None, SPLIT), P(None, SPLIT))
    return jax.shard_map(
        by_columns, mesh=split, in_specs=in_specs, out_specs=out_specs, check_vma=False
    )
```
